32 devices in a mesh: ep: 8 (over y, x, core), dp: 4 (over z).
Axes of the slice: x: 2, y: 2, z: 4, core: 2. Of those that a mesh axis runs over, the one named last changes fastest.
Arguments:
- tokens: bfloat16 [1024, 7168], P('ep', 'dp'), may hold values from -6 to 6
- expert_ids: int32 [1024, 2], P('ep'), may hold values from 0 to 7, all different within a row; in each aligned block of 128 rows (0 to 127, 128 to 255, ...) at most 48 rows name the same one
- gate_probs: float32 [1024, 2], P('ep'), may hold values from 0.1 to 1
- w_gate: bfloat16 [8, 7168, 1024], P('ep', 'dp'), may hold values from -0.0625 to 0.0625
- w_up: bfloat16 [8, 7168, 1024], P('ep', 'dp'), may hold values from -0.0625 to 0.0625
- w_down: bfloat16 [8, 1024, 7168], P('ep', None, 'dp'), may hold values from -0.1875 to 0.1875
- out_grad: bfloat16 [1024, 7168], P('ep', 'dp'), may hold values from -6 to 6
Outputs:
- layer_out: bfloat16 [1024, 7168], P('ep', 'dp')
- token_grad: bfloat16 [1024, 7168], P('ep', 'dp')
The draws below stay inside these ranges and needn't reach their ends.
Inputs may be any that keep to these rules, and one draw needn't show every extreme that they name: `expert_ids`: each row names 2 different experts; among the 128 rows of one aligned block (the tokens of one index of ep) no expert is named more than 48 times, a bound that some block reaches.
All inputs are finite; a program needn't handle non-finite values.
Results may differ from the reference program's by a relative error of at most 0.028.
Values may be sent and summed in bfloat16 or wider, within the bound.
No kernel may reach another device: no remote copies, remote signals or barrier semaphores. Data moves between devices by JAX's collectives and lax.ppermute only.
A program may use at most 64 MiB of HBM per device.

```python
import math
import jax
import jax.numpy as jnp
import numpy as np
from jax import lax

D = 7168
FF = 1024
TOP = 2
TOK_GROUP = 128
TOKENS = 1024
EXPERTS = 8
CAP = 48
N_DP = 4


def shard_levels(key, shape, pieces, least, high):
    def one(axis_at, shards_of):
        heights = jax.random.uniform(jax.random.fold_in(jax.random.fold_in(key, 6), axis_at), (shards_of,), jnp.float32, least / len(pieces), high / len(pieces))
        return jnp.repeat(jnp.exp(heights), shape[axis_at] // shards_of).reshape((-1,) + (1,) * (len(shape) - axis_at - 1))

    factor_of = one(*pieces[0])
    for cut in pieces[1:]:
        factor_of = factor_of * one(*cut)
    return factor_of


def routed_block(rng, own, number, rows, number_of, top, reach, lean):
    sequence = jax.random.permutation(rng, number_of)
    heavy_load, usual = shares(number_of, rows * top, reach, lean, True), shares(number_of, rows * top, reach, lean, False)
    places = jnp.arange(number_of)

    def named(lengths, rotation):
        used = int((lengths > 0).sum())
        fixed = max(1, used // 4)
        passed = fixed + (places - fixed + rotation * (used - fixed)) % max(1, number_of - fixed)
        return jnp.zeros((number_of,), jnp.int32).at[sequence[jnp.where(places < fixed, places, passed)]].set(jnp.asarray(lengths, jnp.int32))

    lengths = jnp.where(number % 4 == 0, named(heavy_load, number // 4), named(usual, number - number // 4 - 1))
    mixed = jax.random.permutation(jax.random.fold_in(own, 3), number_of)
    giver, sink = mixed[0:number_of // 2 * 2:2], mixed[1:number_of // 2 * 2:2]
    slack = jnp.minimum(lengths[giver] - 1, reach - lengths[sink]) // 2
    slack = jnp.where((giver == sequence[0]) | (sink == sequence[0]) | (lengths[sink] == 0), 0, jnp.maximum(slack, 0))
    passed = jax.random.randint(jax.random.fold_in(own, 4), (number_of // 2,), 0, 1 << 20) % (slack + 1)
    lengths = lengths.at[giver].add(-passed).at[sink].add(passed)
    items = jnp.searchsorted(jnp.cumsum(lengths), jnp.arange(rows * top), side="right").astype(jnp.int32)
    listing = items.reshape(top, rows).T
    listing = listing[jax.random.permutation(jax.random.fold_in(own, 1), rows)]
    rotation = jax.random.randint(jax.random.fold_in(own, 2), (rows, 1), 0, top)
    return jnp.take_along_axis(listing, (jnp.arange(top)[None, :] + rotation) % top, axis=1)


def shares(count, total, most, lean, full):
    weights = [(1 << 20) // math.isqrt(grade ** lean) + 1 for grade in range(1, count + 1)]
    largest = most if full else min(most, max(-(-total // count), total * weights[0] // sum(weights)))
    least = 1 if total - largest >= count - 1 else 0
    given, surplus = [largest] + [least] * (count - 1), total - largest - least * (count - 1)
    while surplus > 0:
        candidates = [i for i in range(1, count) if given[i] < largest] or [i for i in range(1, count) if given[i] < most]
        pool, remaining = sum([weights[i] for i in candidates]), surplus
        for i in candidates:
            addition = min(most - given[i], max(1, remaining * weights[i] // pool), surplus)
            given[i] = given[i] + addition
            surplus = surplus - addition
    return np.array(given)


def centred(key, dims, deviation, limit, pieces=(), dtype=jnp.bfloat16):
    level = shard_levels(key, dims, pieces, -0.22, 0.18) if pieces else 1.0
    drawn = jax.random.normal(key, dims, jnp.float32) * deviation * level
    return jnp.minimum(jnp.maximum(drawn, -limit), limit).astype(dtype)


def setup_inputs(seed: int = 0) -> dict:
    seeds = jax.random.split(jax.random.key(seed), 8)
    tokens = centred(seeds[0], (TOKENS, D), 1.0, 6.0, ((0, 8), (1, 4)))
    expert_ids_keys = jax.random.split(jax.random.fold_in(seeds[1], 1), TOKENS // TOK_GROUP)
    expert_ids_turns = jax.random.permutation(jax.random.fold_in(seeds[1], 3), TOKENS // TOK_GROUP)
    expert_ids = jax.vmap(lambda own, number: routed_block(jax.random.fold_in(seeds[1], 2), own, number, TOK_GROUP, EXPERTS, TOP, CAP, 2))(expert_ids_keys, expert_ids_turns).reshape((TOKENS, TOP))
    gate_probs = jnp.clip(jnp.exp(math.log(1.0) - 2.3025851 * jax.random.uniform(seeds[2], (TOKENS, TOP), jnp.float32) ** shard_levels(seeds[2], (TOKENS, TOP), ((0, 8),), -0.2, 0.2)), 0.1, 1.0)
    w_gate = centred(seeds[3], (EXPERTS, D, FF), D ** -0.5, 0.0625, ((0, 8), (1, 4)))
    w_up = centred(seeds[4], (EXPERTS, D, FF), D ** -0.5, 0.0625, ((0, 8), (1, 4)))
    w_down = centred(seeds[5], (EXPERTS, FF, D), FF ** -0.5, 0.1875, ((0, 8), (2, 4)))
    out_grad = centred(seeds[6], (TOKENS, D), 1.0, 6.0, ((0, 8), (1, 4)))
    return dict(tokens=tokens, expert_ids=expert_ids, gate_probs=gate_probs, w_gate=w_gate, w_up=w_up, w_down=w_down, out_grad=out_grad)


def route_tables(group_ids, group_probs, num_experts, capacity):
    group_len = group_ids.shape[0]
    assign_len = group_len * group_ids.shape[1]
    flat_ids = group_ids.reshape(assign_len).astype(jnp.int32)
    same_expert = flat_ids[:, None] == flat_ids[None, :]
    earlier_mask = lax.broadcasted_iota(jnp.int32, (assign_len, assign_len), 1) < lax.broadcasted_iota(jnp.int32, (assign_len, assign_len), 0)
    slot_index = jnp.sum((same_expert & earlier_mask).astype(jnp.int32), axis=1)
    position = (flat_ids * capacity + slot_index).astype(jnp.int32)
    onehot = (lax.broadcasted_iota(jnp.int32, (assign_len, num_experts * capacity), 1) == position[:, None]).astype(jnp.float32)
    token_map = ((lax.broadcasted_iota(jnp.int32, (assign_len, group_len), 0) // group_ids.shape[1]) == lax.broadcasted_iota(jnp.int32, (assign_len, group_len), 1)).astype(jnp.float32)
    weighted = onehot * group_probs.reshape(assign_len)[:, None].astype(jnp.float32)
    combine_map = jnp.dot(token_map.T, weighted, precision=lax.Precision.HIGHEST)
    dispatch_map = jnp.dot(token_map.T, onehot, precision=lax.Precision.HIGHEST)
    return combine_map, dispatch_map


def rounded(value):
    return lax.optimization_barrier(value.astype(jnp.bfloat16)).astype(jnp.float32)


def expert_pass(rows, grad_rows, gate_weight, up_weight, down_weight):
    count = rows.shape[0] * rows.shape[1]
    rows_flat = rows.reshape(count, D)
    grads_flat = grad_rows.reshape(count, D)
    width = D // N_DP
    gate_val = jnp.zeros((count, FF), jnp.float32)
    up_val = jnp.zeros((count, FF), jnp.float32)
    d_hidden = jnp.zeros((count, FF), jnp.float32)
    for slice_idx in range(N_DP):
        lower = slice_idx * width
        upper = lower + width
        gate_val = gate_val + rounded(jnp.dot(rows_flat[:, lower:upper], gate_weight[lower:upper], preferred_element_type=jnp.float32))
        up_val = up_val + rounded(jnp.dot(rows_flat[:, lower:upper], up_weight[lower:upper], preferred_element_type=jnp.float32))
        d_hidden = d_hidden + rounded(jnp.dot(grads_flat[:, lower:upper], down_weight[:, lower:upper].T, preferred_element_type=jnp.float32))
    sigmoid_val = jax.nn.sigmoid(gate_val)
    activated = gate_val * sigmoid_val
    hidden = (activated * up_val).astype(jnp.bfloat16)
    expert_out = jnp.dot(hidden, down_weight, preferred_element_type=jnp.float32).astype(jnp.bfloat16)
    d_gate = (d_hidden * up_val * sigmoid_val * (1.0 + gate_val * (1.0 - sigmoid_val))).astype(jnp.bfloat16)
    d_up = (d_hidden * activated).astype(jnp.bfloat16)
    input_out = jnp.dot(d_gate, gate_weight.T, preferred_element_type=jnp.float32)
    input_out = input_out + jnp.dot(d_up, up_weight.T, preferred_element_type=jnp.float32)
    return expert_out.reshape(rows.shape), input_out.astype(jnp.bfloat16).reshape(rows.shape)


def reference(tokens, expert_ids, gate_probs, w_gate, w_up, w_down, out_grad):
    groups = TOKENS // TOK_GROUP
    group_tokens = tokens.reshape(groups, TOK_GROUP, D)
    group_grads = out_grad.reshape(groups, TOK_GROUP, D)
    combine_map, dispatch_map = jax.vmap(lambda ids_g, probs_g: route_tables(ids_g, probs_g, EXPERTS, CAP))(
        expert_ids.reshape(groups, TOK_GROUP, TOP), gate_probs.reshape(groups, TOK_GROUP, TOP))
    rows = jnp.einsum("gtp,gtd->gpd", dispatch_map, group_tokens.astype(jnp.float32), precision=lax.Precision.HIGHEST).astype(jnp.bfloat16)
    grad_rows = jnp.einsum("gtp,gtd->gpd", combine_map, group_grads.astype(jnp.float32), precision=lax.Precision.HIGHEST).astype(jnp.bfloat16)
    rows = rows.reshape(groups, EXPERTS, CAP, D).transpose(1, 0, 2, 3)
    grad_rows = grad_rows.reshape(groups, EXPERTS, CAP, D).transpose(1, 0, 2, 3)
    expert_out, input_out = lax.map(lambda packed: expert_pass(*packed), (rows, grad_rows, w_gate, w_up, w_down))
    expert_out = expert_out.transpose(1, 0, 2, 3).reshape(groups, EXPERTS * CAP, D)
    input_out = input_out.transpose(1, 0, 2, 3).reshape(groups, EXPERTS * CAP, D)
    layer_out = jnp.einsum("gtp,gpd->gtd", combine_map, expert_out.astype(jnp.float32), precision=lax.Precision.HIGHEST).astype(jnp.bfloat16)
    token_grad = jnp.einsum("gtp,gpd->gtd", dispatch_map, input_out.astype(jnp.float32), precision=lax.Precision.HIGHEST).astype(jnp.bfloat16)
    return layer_out.reshape(TOKENS, D), token_grad.reshape(TOKENS, D)
```

```python
import functools

import jax
import jax.numpy as jnp
from jax import lax
from jax.experimental import pallas as pl
from jax.experimental.pallas import tpu as pltpu
from jax.sharding import PartitionSpec as P

TOP = 2
BF16 = jnp.bfloat16
F32 = jnp.float32

ROW_SETS = ((0,), (1, 2, 3))


def route_tables(group_ids, group_probs, num_experts, capacity):
    group_len = group_ids.shape[0]
    assign_len = group_len * group_ids.shape[1]
    flat_ids = group_ids.reshape(assign_len)
    same_expert = flat_ids[:, None] == flat_ids[None, :]
    earlier_mask = lax.broadcasted_iota(
        jnp.int32, (assign_len, assign_len), 1
    ) < lax.broadcasted_iota(jnp.int32, (assign_len, assign_len), 0)
    slot_index = jnp.sum((same_expert & earlier_mask).astype(jnp.int32), axis=1)
    position = flat_ids * capacity + slot_index
    onehot = (
        lax.broadcasted_iota(jnp.int32, (assign_len, num_experts * capacity), 1)
        == position[:, None]
    ).astype(jnp.float32)
    token_map = (
        lax.broadcasted_iota(jnp.int32, (assign_len, group_len), 0) // group_ids.shape[1]
        == lax.broadcasted_iota(jnp.int32, (assign_len, group_len), 1)
    ).astype(jnp.float32)
    weighted = onehot * group_probs.reshape(assign_len)[:, None]
    combine_map = jnp.dot(token_map.T, weighted, precision=lax.Precision.HIGHEST)
    dispatch_map = jnp.dot(token_map.T, onehot, precision=lax.Precision.HIGHEST)
    return (combine_map, dispatch_map)


def rounded(value):
    return lax.optimization_barrier(value.astype(jnp.bfloat16)).astype(jnp.float32)


def move_rows(slots):
    return lax.all_to_all(slots, "ep", split_axis=0, concat_axis=0, tiled=True)


def local_any(tokens, expert_ids, gate_probs, w_gate, w_up, w_down, out_grad):
    num_experts = lax.axis_size("ep")
    group_len = expert_ids.shape[0]
    capacity = 3 * ((group_len * TOP + 2 * num_experts - 1) // (2 * num_experts))
    combine_map, dispatch_map = route_tables(expert_ids, gate_probs, num_experts, capacity)
    slot_count = num_experts * capacity
    feature_width = tokens.shape[1]
    send_rows = lax.dot_general(
        dispatch_map.astype(jnp.bfloat16),
        tokens,
        (((0,), (0,)), ((), ())),
        preferred_element_type=jnp.float32,
    )
    send_rows = send_rows.astype(jnp.bfloat16).reshape(num_experts, capacity, feature_width)
    grad_send = lax.dot_general(
        combine_map,
        out_grad.astype(jnp.float32),
        (((0,), (0,)), ((), ())),
        precision=lax.Precision.HIGHEST,
    )
    grad_send = grad_send.astype(jnp.bfloat16).reshape(num_experts, capacity, feature_width)
    inputs = move_rows(send_rows).reshape(slot_count, feature_width)
    grad_rows = None
    gate_weight = w_gate[0]
    up_weight = w_up[0]
    down_weight = w_down[0]
    gate_part = rounded(jnp.dot(inputs, gate_weight, preferred_element_type=jnp.float32))
    up_part = rounded(jnp.dot(inputs, up_weight, preferred_element_type=jnp.float32))
    gate_slice, up_slice = (
        lax.psum_scatter(
            gate_part.astype(jnp.bfloat16), "dp", scatter_dimension=1, tiled=True
        ).astype(jnp.float32),
        lax.psum_scatter(
            up_part.astype(jnp.bfloat16), "dp", scatter_dimension=1, tiled=True
        ).astype(jnp.float32),
    )
    hidden_slice = (gate_slice * jax.nn.sigmoid(gate_slice) * up_slice).astype(jnp.bfloat16)
    hidden = lax.all_gather(hidden_slice, "dp", axis=1, tiled=True)
    expert_out = jnp.dot(hidden, down_weight, preferred_element_type=jnp.float32).astype(
        jnp.bfloat16
    )
    returned = move_rows(expert_out.reshape(num_experts, capacity, feature_width)).reshape(
        slot_count, feature_width
    )
    layer_out = jnp.dot(
        combine_map, returned.astype(jnp.float32), precision=lax.Precision.HIGHEST
    ).astype(jnp.bfloat16)
    grad_rows = move_rows(grad_send).reshape(slot_count, feature_width)
    d_part = rounded(
        lax.dot_general(
            grad_rows, down_weight, (((1,), (1,)), ((), ())), preferred_element_type=jnp.float32
        )
    )
    d_hidden = lax.psum_scatter(
        d_part.astype(jnp.bfloat16), "dp", scatter_dimension=1, tiled=True
    ).astype(jnp.float32)
    sigmoid_val = jax.nn.sigmoid(gate_slice)
    activated = gate_slice * sigmoid_val
    d_gate = (d_hidden * up_slice * sigmoid_val * (1.0 + gate_slice * (1.0 - sigmoid_val))).astype(
        jnp.bfloat16
    )
    d_up = (d_hidden * activated).astype(jnp.bfloat16)
    whole_gate, whole_up = (
        lax.all_gather(d_gate, "dp", axis=1, tiled=True),
        lax.all_gather(d_up, "dp", axis=1, tiled=True),
    )
    input_part = lax.dot_general(
        whole_gate, gate_weight, (((1,), (1,)), ((), ())), preferred_element_type=jnp.float32
    )
    input_part = input_part + lax.dot_general(
        whole_up, up_weight, (((1,), (1,)), ((), ())), preferred_element_type=jnp.float32
    )
    input_out = move_rows(
        input_part.astype(jnp.bfloat16).reshape(num_experts, capacity, feature_width)
    ).reshape(slot_count, feature_width)
    token_grad = jnp.dot(
        dispatch_map, input_out.astype(jnp.float32), precision=lax.Precision.HIGHEST
    ).astype(jnp.bfloat16)
    return (layer_out, token_grad)


def order(n):
    places = [0]
    while len(places) < n:
        step = n // (2 * len(places))
        places = places + [p + step for p in places]
    return places


def swap(value, axis, mask):
    size = lax.axis_size(axis)
    return lax.ppermute(value, axis, [(i, i ^ mask) for i in range(size)])


def route_rows(meta, me, stride, count):
    tokens = meta.shape[1]
    padded = -(-count // 8) * 8
    place = lax.broadcasted_iota(jnp.int32, (padded, tokens), 0)
    target = jnp.where(place < count, me ^ (place * stride), -1).astype(F32)
    first, second = meta[0:1, :] == target, meta[1:2, :] == target
    hit = first | second
    weight = jnp.where(first, meta[2:3, :], 0.0) + jnp.where(second, meta[3:4, :], 0.0)
    before = lax.broadcasted_iota(jnp.int32, (tokens, tokens), 0) < lax.broadcasted_iota(
        jnp.int32, (tokens, tokens), 1
    )
    earlier = jnp.dot(
        jnp.where(hit, 1.0, 0.0).astype(BF16),
        jnp.where(before, 1.0, 0.0).astype(BF16),
        preferred_element_type=F32,
    )
    return jnp.where(hit, earlier, -1.0), weight


def slot_map(slots, weights, r, capacity):
    tokens = slots.shape[1]
    slot = lax.broadcasted_iota(jnp.int32, (capacity, tokens), 0).astype(F32)
    return jnp.where(slots[r : r + 1, :] == slot, weights[r : r + 1, :], 0.0)


def gather_kernel(experts, capacity, weighted, s_ref, meta_ref, x_ref, own_ref, away_ref, map_ref, scale_ref):
    chips = experts // 2

    @pl.when(pl.program_id(0) == 0)
    def _():
        slots, weights = route_rows(meta_ref[...], s_ref[0], 1, experts)
        ones = jnp.ones_like(weights)
        for q in range(2):
            for k in range(chips):
                at = (q * chips + k) * capacity
                map_ref[at : at + capacity, :] = slot_map(slots, ones, 2 * k + q, capacity).astype(BF16)
                if weighted:
                    scale_ref[at : at + capacity, :] = jnp.sum(
                        slot_map(slots, weights, 2 * k + q, capacity), axis=1, keepdims=True
                    )

    x = x_ref[...]
    half = chips * capacity
    for q, out_ref in enumerate((own_ref, away_ref)):
        rows = jnp.dot(map_ref[q * half : (q + 1) * half, :], x, preferred_element_type=F32)
        if weighted:
            rows = rows * scale_ref[q * half : (q + 1) * half, :]
        out_ref[...] = rows.astype(BF16)


def gather_rows(scalars, meta, x, experts, capacity, weighted):
    tokens, width = x.shape
    column = width // 2
    half = experts // 2 * capacity
    return pl.pallas_call(
        functools.partial(gather_kernel, experts, capacity, weighted),
        grid_spec=pltpu.PrefetchScalarGridSpec(
            num_scalar_prefetch=1,
            grid=(width // column,),
            in_specs=[
                pl.BlockSpec(meta.shape, lambda j, s: (0, 0)),
                pl.BlockSpec((tokens, column), lambda j, s: (0, j)),
            ],
            out_specs=[pl.BlockSpec((half, column), lambda j, s: (0, j))] * 2,
            scratch_shapes=[
                pltpu.VMEM((2 * half, tokens), BF16),
                pltpu.VMEM((2 * half, 1), F32),
            ],
        ),
        out_shape=[jax.ShapeDtypeStruct((half, width), BF16)] * 2,
        cost_estimate=pl.CostEstimate(
            flops=4 * half * tokens * width, bytes_accessed=6 * half * width, transcendentals=0
        ),
        name="gather_weighted" if weighted else "gather_plain",
    )(scalars, meta, x)


def combine_kernel(chips, capacity, group, weighted, s_ref, meta_ref, *refs):
    row_refs, out_ref, map_ref = refs[:chips], refs[chips], refs[chips + 1]
    pieces = map_ref.shape[0]

    @pl.when(pl.program_id(0) == 0)
    def _():
        slots, weights = route_rows(meta_ref[...], s_ref[0], 2, chips)
        if not weighted:
            weights = jnp.ones_like(weights)
        left = jnp.concatenate([slot_map(slots, weights, k, capacity) for k in range(chips)], axis=0).T
        for i in range(pieces):
            piece = left.astype(BF16)
            map_ref[i, :, :] = piece
            left = left - piece.astype(F32)

    rows = jnp.concatenate([r[group * capacity : (group + 1) * capacity, :] for r in row_refs], axis=0)
    total = jnp.dot(map_ref[pieces - 1], rows, preferred_element_type=F32)
    for i in reversed(range(pieces - 1)):
        total = total + jnp.dot(map_ref[i], rows, preferred_element_type=F32)
    out_ref[...] = total.astype(out_ref.dtype)


def combine_rows(scalars, meta, returned, capacity, group, weighted, dtype):
    chips, width = len(returned), returned[0].shape[1]
    tokens = meta.shape[1]
    column = width // 2
    pieces = 3 if weighted else 1
    return pl.pallas_call(
        functools.partial(combine_kernel, chips, capacity, group, weighted),
        grid_spec=pltpu.PrefetchScalarGridSpec(
            num_scalar_prefetch=1,
            grid=(width // column,),
            in_specs=[pl.BlockSpec(meta.shape, lambda j, s: (0, 0))]
            + [pl.BlockSpec((2 * capacity, column), lambda j, s: (0, j))] * chips,
            out_specs=pl.BlockSpec((tokens, column), lambda j, s: (0, j)),
            scratch_shapes=[pltpu.VMEM((pieces, tokens, chips * capacity), BF16)],
        ),
        out_shape=jax.ShapeDtypeStruct((tokens, width), dtype),
        cost_estimate=pl.CostEstimate(
            flops=2 * pieces * tokens * chips * capacity * width,
            bytes_accessed=4 * chips * capacity * width,
            transcendentals=0,
        ),
        name=f"combine_{group}_{pieces}",
    )(scalars, meta, *returned)


def part_kernel(count, contract, s_ref, *refs):
    x_refs, w_refs, out_ref = refs[:count], refs[count:-1], refs[-1]
    at = 0
    for x_ref in x_refs:
        rows = x_ref.shape[0]
        for i, w_ref in enumerate(w_refs):
            block = out_ref.shape[2] // len(w_refs)
            out_ref[0, at : at + rows, i * block : (i + 1) * block] = lax.dot_general(
                x_ref[...], w_ref[0], (((1,), (contract,)), ((), ())), preferred_element_type=F32
            ).astype(BF16)
        at += rows


def part_blocks(scalars, xs, ws, contract, first, count, n, name):
    width = xs[0].shape[1]
    block = ws[0].shape[2 if contract == 0 else 1] // n
    rows = sum(x.shape[0] for x in xs)
    if contract == 0:
        w_spec = pl.BlockSpec((1, width, block), lambda j, s: (0, 0, s[1 + first + j]))
    else:
        w_spec = pl.BlockSpec((1, block, width), lambda j, s: (0, s[1 + first + j], 0))
    return pl.pallas_call(
        functools.partial(part_kernel, len(xs), contract),
        grid_spec=pltpu.PrefetchScalarGridSpec(
            num_scalar_prefetch=1,
            grid=(count,),
            in_specs=[pl.BlockSpec(x.shape, lambda j, s: (0, 0)) for x in xs] + [w_spec] * len(ws),
            out_specs=pl.BlockSpec((1, rows, block * len(ws)), lambda j, s: (j, 0, 0)),
        ),
        out_shape=jax.ShapeDtypeStruct((count, rows, block * len(ws)), BF16),
        cost_estimate=pl.CostEstimate(
            flops=2 * rows * width * block * len(ws) * count,
            bytes_accessed=2 * (rows * width + width * block * len(ws) * count),
            transcendentals=0,
        ),
        name=name,
    )(scalars, *xs, *ws)


def whole_kernel(count, outs, block, contract, s_ref, *refs):
    h_refs, rest = refs[:count], refs[count:]
    w_refs, out_refs = rest[: len(rest) - outs], rest[len(rest) - outs :]
    total = None
    at = 0
    for h_ref in h_refs:
        for b in range(h_ref.shape[0]):
            start = pl.multiple_of(s_ref[1 + at] * block, block)
            for i, w_ref in enumerate(w_refs):
                h = h_ref[b, :, i * block : (i + 1) * block]
                w = w_ref[0, pl.ds(start, block), :] if contract == 0 else w_ref[0, :, pl.ds(start, block)]
                part = lax.dot_general(h, w, (((1,), (contract,)), ((), ())), preferred_element_type=F32)
                total = part if total is None else total + part
            at += 1
    rows = total.shape[0] // outs
    for i, out_ref in enumerate(out_refs):
        out_ref[...] = total[i * rows : (i + 1) * rows, :].astype(BF16)


def whole_product(scalars, pieces, ws, contract, outs, n, name):
    width = ws[0].shape[2 if contract == 0 else 1]
    hidden = ws[0].shape[1 if contract == 0 else 2]
    block = hidden // n
    rows = pieces[0].shape[1]
    column = 256 if width % 256 == 0 else width
    if contract == 0:
        w_spec = pl.BlockSpec((1, hidden, column), lambda j, s: (0, 0, j))
    else:
        w_spec = pl.BlockSpec((1, column, hidden), lambda j, s: (0, j, 0))
    return pl.pallas_call(
        functools.partial(whole_kernel, len(pieces), outs, block, contract),
        grid_spec=pltpu.PrefetchScalarGridSpec(
            num_scalar_prefetch=1,
            grid=(width // column,),
            in_specs=[pl.BlockSpec(p.shape, lambda j, s: (0, 0, 0)) for p in pieces] + [w_spec] * len(ws),
            out_specs=[pl.BlockSpec((rows // outs, column), lambda j, s: (0, j))] * outs,
        ),
        out_shape=[jax.ShapeDtypeStruct((rows // outs, width), BF16)] * outs,
        cost_estimate=pl.CostEstimate(
            flops=2 * rows * width * hidden * len(ws),
            bytes_accessed=2 * (rows * width + hidden * width * len(ws)),
            transcendentals=0,
        ),
        name=name,
    )(scalars, *pieces, *ws)


def sum_blocks(make, n):
    held = n // 2
    sent = make(held, held)
    addends = [swap(sent, "dp", 1), make(0, held)]
    mask = 2
    while mask < n:
        held //= 2
        leaving = sum(a[held:].astype(F32) for a in addends).astype(BF16)
        addends = [a[:held] for a in addends] + [swap(leaving, "dp", mask)]
        mask *= 2
    return sum(a[0].astype(F32) for a in addends)


def spread_blocks(mine, n):
    pieces = [mine[None]]
    mask = n // 2
    while mask:
        pieces.append(swap(pieces[0] if len(pieces) == 1 else jnp.concatenate(pieces, axis=0), "dp", mask))
        mask //= 2
    return pieces


def local_paired(tokens, expert_ids, gate_probs, w_gate, w_up, w_down, out_grad):
    experts, n = lax.axis_size("ep"), lax.axis_size("dp")
    chips = experts // 2
    group_len = expert_ids.shape[0]
    capacity = 3 * ((group_len * TOP + 2 * experts - 1) // (2 * experts))
    z = lax.axis_index("dp")
    scalars = jnp.stack([lax.axis_index("ep")] + [z ^ p for p in order(n)]).astype(jnp.int32)
    meta = jnp.concatenate([expert_ids.T.astype(F32), gate_probs.T], axis=0)
    meta_away = swap(meta, "ep", 1)

    def send_out(x, weighted):
        own, away = gather_rows(scalars, meta, x, experts, capacity, weighted)
        came = swap(away, "ep", 1)
        arrived = {}
        for k in range(chips):
            part = slice(k * capacity, (k + 1) * capacity)
            both = jnp.concatenate([own[part], came[part]], axis=0)
            arrived[k] = swap(both, "ep", 2 * k) if k else both
        return arrived

    rows = send_out(tokens, False)
    grads = send_out(out_grad, True)

    sets = [tuple(k for k in ks if k < chips) for ks in ROW_SETS]
    sums = []
    for ks in sets:
        sums.append(
            sum_blocks(
                lambda first, count: part_blocks(
                    scalars, [rows[k] for k in ks], [w_gate, w_up], 0, first, count, n, "gate_up"
                ),
                n,
            )
        )
    hidden_pieces, back = [], []
    block = w_gate.shape[2] // n
    for ks, total in zip(sets, sums):
        gate, up = total[:, :block], total[:, block:]
        sigmoid = jax.nn.sigmoid(gate)
        hidden_pieces.append(spread_blocks((gate * sigmoid * up).astype(BF16), n))
    for ks, total in zip(sets, sums):
        gate, up = total[:, :block], total[:, block:]
        d_hidden = sum_blocks(
            lambda first, count: part_blocks(
                scalars, [grads[k] for k in ks], [w_down], 1, first, count, n, "d_hidden"
            ),
            n,
        )
        sigmoid = jax.nn.sigmoid(gate)
        d_gate = d_hidden * up * sigmoid * (1.0 + gate * (1.0 - sigmoid))
        d_up = d_hidden * (gate * sigmoid)
        back.append(jnp.concatenate([d_gate, d_up], axis=1).astype(BF16))

    def bring_back(ks, made):
        return {k: swap(m, "ep", 2 * k) if k else m for k, m in zip(ks, made)}

    out_back, in_back = {}, {}
    for ks, pieces in reversed(list(zip(sets, hidden_pieces))):
        made = whole_product(scalars, pieces, [w_down], 0, len(ks), n, "expert_out")
        out_back.update(bring_back(ks, made))
    for ks, mine in reversed(list(zip(sets, back))):
        made = whole_product(scalars, spread_blocks(mine, n), [w_gate, w_up], 1, len(ks), n, "input_out")
        in_back.update(bring_back(ks, made))

    def finish(returned, weighted):
        returned = [returned[k] for k in range(chips)]
        away = combine_rows(scalars, meta_away, returned, capacity, 1, weighted, BF16)
        came = swap(away, "ep", 1)
        own = combine_rows(scalars, meta, returned, capacity, 0, weighted, F32)
        return (own + came.astype(F32)).astype(BF16)

    return finish(out_back, True), finish(in_back, False)


def paired(experts, n, group_len, hidden):
    capacity = 3 * ((group_len * TOP + 2 * experts - 1) // (2 * experts))
    whole = experts & (experts - 1) == 0 and n & (n - 1) == 0 and min(experts, n) > 1
    return whole and experts <= 8 and hidden % (128 * n) == 0 and capacity % 16 == 0


def local(tokens, expert_ids, gate_probs, w_gate, w_up, w_down, out_grad):
    fits = paired(lax.axis_size("ep"), lax.axis_size("dp"), expert_ids.shape[0], w_gate.shape[2])
    step = local_paired if fits else local_any
    return step(tokens, expert_ids, gate_probs, w_gate, w_up, w_down, out_grad)


def solution(mesh):
    return jax.shard_map(
        local,
        mesh=mesh,
        in_specs=(
            P("ep", "dp"),
            P("ep", None),
            P("ep", None),
            P("ep", "dp", None),
            P("ep", "dp", None),
            P("ep", None, "dp"),
            P("ep", "dp"),
        ),
        out_specs=(P("ep", "dp"), P("ep", "dp")),
        check_vma=False,
    )
```

```python
import functools

import jax
import jax.numpy as jnp
from jax import lax
from jax.experimental import pallas as pl
from jax.experimental.pallas import tpu as pltpu
from jax.sharding import PartitionSpec as P

TOP = 2
BF16 = jnp.bfloat16
F32 = jnp.float32

ROW_SETS = ((0,), (1, 2, 3))
SCRATCH_BYTES = 12 << 20


def route_tables(group_ids, group_probs, num_experts, capacity):
    group_len = group_ids.shape[0]
    assign_len = group_len * group_ids.shape[1]
    flat_ids = group_ids.reshape(assign_len)
    same_expert = flat_ids[:, None] == flat_ids[None, :]
    earlier_mask = lax.broadcasted_iota(
        jnp.int32, (assign_len, assign_len), 1
    ) < lax.broadcasted_iota(jnp.int32, (assign_len, assign_len), 0)
    slot_index = jnp.sum((same_expert & earlier_mask).astype(jnp.int32), axis=1)
    position = flat_ids * capacity + slot_index
    onehot = (
        lax.broadcasted_iota(jnp.int32, (assign_len, num_experts * capacity), 1)
        == position[:, None]
    ).astype(jnp.float32)
    token_map = (
        lax.broadcasted_iota(jnp.int32, (assign_len, group_len), 0) // group_ids.shape[1]
        == lax.broadcasted_iota(jnp.int32, (assign_len, group_len), 1)
    ).astype(jnp.float32)
    weighted = onehot * group_probs.reshape(assign_len)[:, None]
    combine_map = jnp.dot(token_map.T, weighted, precision=lax.Precision.HIGHEST)
    dispatch_map = jnp.dot(token_map.T, onehot, precision=lax.Precision.HIGHEST)
    return (combine_map, dispatch_map)


def rounded(value):
    return lax.optimization_barrier(value.astype(jnp.bfloat16)).astype(jnp.float32)


def move_rows(slots):
    return lax.all_to_all(slots, "ep", split_axis=0, concat_axis=0, tiled=True)


def local_any(tokens, expert_ids, gate_probs, w_gate, w_up, w_down, out_grad):
    num_experts = lax.axis_size("ep")
    group_len = expert_ids.shape[0]
    capacity = 3 * ((group_len * TOP + 2 * num_experts - 1) // (2 * num_experts))
    combine_map, dispatch_map = route_tables(expert_ids, gate_probs, num_experts, capacity)
    slot_count = num_experts * capacity
    feature_width = tokens.shape[1]
    send_rows = lax.dot_general(
        dispatch_map.astype(jnp.bfloat16),
        tokens,
        (((0,), (0,)), ((), ())),
        preferred_element_type=jnp.float32,
    )
    send_rows = send_rows.astype(jnp.bfloat16).reshape(num_experts, capacity, feature_width)
    grad_send = lax.dot_general(
        combine_map,
        out_grad.astype(jnp.float32),
        (((0,), (0,)), ((), ())),
        precision=lax.Precision.HIGHEST,
    )
    grad_send = grad_send.astype(jnp.bfloat16).reshape(num_experts, capacity, feature_width)
    inputs = move_rows(send_rows).reshape(slot_count, feature_width)
    grad_rows = None
    gate_weight = w_gate[0]
    up_weight = w_up[0]
    down_weight = w_down[0]
    gate_part = rounded(jnp.dot(inputs, gate_weight, preferred_element_type=jnp.float32))
    up_part = rounded(jnp.dot(inputs, up_weight, preferred_element_type=jnp.float32))
    gate_slice, up_slice = (
        lax.psum_scatter(
            gate_part.astype(jnp.bfloat16), "dp", scatter_dimension=1, tiled=True
        ).astype(jnp.float32),
        lax.psum_scatter(
            up_part.astype(jnp.bfloat16), "dp", scatter_dimension=1, tiled=True
        ).astype(jnp.float32),
    )
    hidden_slice = (gate_slice * jax.nn.sigmoid(gate_slice) * up_slice).astype(jnp.bfloat16)
    hidden = lax.all_gather(hidden_slice, "dp", axis=1, tiled=True)
    expert_out = jnp.dot(hidden, down_weight, preferred_element_type=jnp.float32).astype(
        jnp.bfloat16
    )
    returned = move_rows(expert_out.reshape(num_experts, capacity, feature_width)).reshape(
        slot_count, feature_width
    )
    layer_out = jnp.dot(
        combine_map, returned.astype(jnp.float32), precision=lax.Precision.HIGHEST
    ).astype(jnp.bfloat16)
    grad_rows = move_rows(grad_send).reshape(slot_count, feature_width)
    d_part = rounded(
        lax.dot_general(
            grad_rows, down_weight, (((1,), (1,)), ((), ())), preferred_element_type=jnp.float32
        )
    )
    d_hidden = lax.psum_scatter(
        d_part.astype(jnp.bfloat16), "dp", scatter_dimension=1, tiled=True
    ).astype(jnp.float32)
    sigmoid_val = jax.nn.sigmoid(gate_slice)
    activated = gate_slice * sigmoid_val
    d_gate = (d_hidden * up_slice * sigmoid_val * (1.0 + gate_slice * (1.0 - sigmoid_val))).astype(
        jnp.bfloat16
    )
    d_up = (d_hidden * activated).astype(jnp.bfloat16)
    whole_gate, whole_up = (
        lax.all_gather(d_gate, "dp", axis=1, tiled=True),
        lax.all_gather(d_up, "dp", axis=1, tiled=True),
    )
    input_part = lax.dot_general(
        whole_gate, gate_weight, (((1,), (1,)), ((), ())), preferred_element_type=jnp.float32
    )
    input_part = input_part + lax.dot_general(
        whole_up, up_weight, (((1,), (1,)), ((), ())), preferred_element_type=jnp.float32
    )
    input_out = move_rows(
        input_part.astype(jnp.bfloat16).reshape(num_experts, capacity, feature_width)
    ).reshape(slot_count, feature_width)
    token_grad = jnp.dot(
        dispatch_map, input_out.astype(jnp.float32), precision=lax.Precision.HIGHEST
    ).astype(jnp.bfloat16)
    return (layer_out, token_grad)


def order(n):
    places = [0]
    while len(places) < n:
        step = n // (2 * len(places))
        places = places + [p + step for p in places]
    return places


def swap(value, axis, mask):
    size = lax.axis_size(axis)
    return lax.ppermute(value, axis, [(i, i ^ mask) for i in range(size)])


def route_rows(meta, me, stride, count):
    tokens = meta.shape[1]
    padded = -(-count // 8) * 8
    place = lax.broadcasted_iota(jnp.int32, (padded, tokens), 0)
    target = jnp.where(place < count, me ^ (place * stride), -1).astype(F32)
    first, second = meta[0:1, :] == target, meta[1:2, :] == target
    hit = first | second
    weight = jnp.where(first, meta[2:3, :], 0.0) + jnp.where(second, meta[3:4, :], 0.0)
    before = lax.broadcasted_iota(jnp.int32, (tokens, tokens), 0) < lax.broadcasted_iota(
        jnp.int32, (tokens, tokens), 1
    )
    earlier = jnp.dot(
        jnp.where(hit, 1.0, 0.0).astype(BF16),
        jnp.where(before, 1.0, 0.0).astype(BF16),
        preferred_element_type=F32,
    )
    return jnp.where(hit, earlier, -1.0), weight


def slot_map(slots, weights, r, capacity):
    tokens = slots.shape[1]
    slot = lax.broadcasted_iota(jnp.int32, (capacity, tokens), 0).astype(F32)
    return jnp.where(slots[r : r + 1, :] == slot, weights[r : r + 1, :], 0.0)


VMEM = pl.BlockSpec(memory_space=pltpu.VMEM)
SMEM = pl.BlockSpec(memory_space=pltpu.SMEM)


def whole_call(kernel, out_shape, scratch, flops, moved, name, scalars, *operands):
    return pl.pallas_call(
        kernel,
        in_specs=[SMEM] + [VMEM] * len(operands),
        out_specs=jax.tree.map(lambda _: VMEM, out_shape),
        out_shape=out_shape,
        scratch_shapes=scratch,
        compiler_params=pltpu.CompilerParams(vmem_limit_bytes=SCRATCH_BYTES),
        cost_estimate=pl.CostEstimate(flops=flops, bytes_accessed=moved, transcendentals=0),
        name=name,
    )(scalars, *operands)


def column_step(width):
    return 256 if width % 256 == 0 else width


def gather_kernel(chips, capacity, weighted, s_ref, own_meta, away_meta, own_x, away_x, *refs):
    out_refs, map_ref, scale_ref = refs[:chips], refs[chips], refs[chips + 1]
    half = chips * capacity
    for g, meta_ref in enumerate((own_meta, away_meta)):
        slots, weights = route_rows(meta_ref[...], s_ref[0], 2, chips)
        ones = jnp.ones_like(weights)
        for k in range(chips):
            at = g * half + k * capacity
            map_ref[at : at + capacity, :] = slot_map(slots, ones, k, capacity).astype(BF16)
            if weighted:
                scale_ref[at : at + capacity, :] = jnp.sum(
                    slot_map(slots, weights, k, capacity), axis=1, keepdims=True
                )
    width = own_x.shape[1]
    column = column_step(width)

    def step(j, carry):
        columns = pl.ds(pl.multiple_of(j * column, column), column)
        for g, x_ref in enumerate((own_x, away_x)):
            rows = jnp.dot(map_ref[g * half : (g + 1) * half, :], x_ref[:, columns], preferred_element_type=F32)
            if weighted:
                rows = rows * scale_ref[g * half : (g + 1) * half, :]
            for k in range(chips):
                out_refs[k][g * capacity : (g + 1) * capacity, columns] = rows[
                    k * capacity : (k + 1) * capacity
                ].astype(BF16)
        return carry

    lax.fori_loop(0, width // column, step, 0)


def gather_rows(scalars, metas, xs, chips, capacity, weighted):
    tokens, width = xs[0].shape
    half = chips * capacity
    return whole_call(
        functools.partial(gather_kernel, chips, capacity, weighted),
        [jax.ShapeDtypeStruct((2 * capacity, width), BF16)] * chips,
        [pltpu.VMEM((2 * half, tokens), BF16), pltpu.VMEM((2 * half, 1), F32)],
        4 * half * tokens * width,
        6 * half * width,
        "gather_weighted" if weighted else "gather_plain",
        scalars,
        *metas,
        *xs,
    )


def combine_kernel(chips, capacity, group, weighted, s_ref, meta_ref, *refs):
    row_refs, out_ref = refs[:chips], refs[chips]
    slots, weights = route_rows(meta_ref[...], s_ref[0], 2, chips)
    if not weighted:
        weights = jnp.ones_like(weights)
    left = jnp.concatenate([slot_map(slots, weights, k, capacity) for k in range(chips)], axis=0).T
    pieces = []
    for _ in range(3 if weighted else 1):
        pieces.append(left.astype(BF16))
        left = left - pieces[-1].astype(F32)
    width = out_ref.shape[1]
    column = column_step(width)

    def step(j, carry):
        columns = pl.ds(pl.multiple_of(j * column, column), column)
        rows = jnp.concatenate([r[group * capacity : (group + 1) * capacity, columns] for r in row_refs], axis=0)
        total = None
        for piece in reversed(pieces):
            part = jnp.dot(piece, rows, preferred_element_type=F32)
            total = part if total is None else total + part
        out_ref[:, columns] = total.astype(out_ref.dtype)
        return carry

    lax.fori_loop(0, width // column, step, 0)


def combine_rows(scalars, meta, returned, capacity, group, weighted, dtype):
    chips, width = len(returned), returned[0].shape[1]
    tokens = meta.shape[1]
    return whole_call(
        functools.partial(combine_kernel, chips, capacity, group, weighted),
        jax.ShapeDtypeStruct((tokens, width), dtype),
        [],
        6 * tokens * chips * capacity * width,
        4 * chips * capacity * width,
        f"combine_{group}_{'weighted' if weighted else 'plain'}",
        scalars,
        meta,
        *returned,
    )


def part_kernel(count, contract, first, block, s_ref, *refs):
    x_refs, w_refs, out_ref = refs[:count], refs[count:-1], refs[-1]
    x = jnp.concatenate([r[...] for r in x_refs], axis=0) if count > 1 else x_refs[0][...]
    for j in range(out_ref.shape[0]):
        at = pl.ds(pl.multiple_of(s_ref[1 + first + j] * block, block), block)
        for i, w_ref in enumerate(w_refs):
            w = w_ref[0, :, at] if contract == 0 else w_ref[0, at, :]
            out_ref[j, :, i * block : (i + 1) * block] = lax.dot_general(
                x, w, (((1,), (contract,)), ((), ())), preferred_element_type=F32
            ).astype(BF16)


def part_blocks(scalars, xs, ws, contract, first, count, n, name):
    width = xs[0].shape[1]
    block = ws[0].shape[2 if contract == 0 else 1] // n
    rows = sum(x.shape[0] for x in xs)
    return whole_call(
        functools.partial(part_kernel, len(xs), contract, first, block),
        jax.ShapeDtypeStruct((count, rows, block * len(ws)), BF16),
        [],
        2 * rows * width * block * len(ws) * count,
        2 * (rows * width + width * block * len(ws) * count),
        name,
        scalars,
        *xs,
        *ws,
    )


def whole_kernel(count, outs, block, contract, s_ref, *refs):
    h_refs, rest = refs[:count], refs[count:]
    w_refs, out_refs = rest[: len(rest) - outs], rest[len(rest) - outs :]
    width = out_refs[0].shape[1]
    column = column_step(width)

    def step(j, carry):
        columns = pl.ds(pl.multiple_of(j * column, column), column)
        total = None
        at = 0
        for h_ref in h_refs:
            for b in range(h_ref.shape[0]):
                units = pl.ds(pl.multiple_of(s_ref[1 + at] * block, block), block)
                for i, w_ref in enumerate(w_refs):
                    h = h_ref[b, :, i * block : (i + 1) * block]
                    w = w_ref[0, units, columns] if contract == 0 else w_ref[0, columns, units]
                    part = lax.dot_general(h, w, (((1,), (contract,)), ((), ())), preferred_element_type=F32)
                    total = part if total is None else total + part
                at += 1
        rows = total.shape[0] // outs
        for i, out_ref in enumerate(out_refs):
            out_ref[:, columns] = total[i * rows : (i + 1) * rows, :].astype(BF16)
        return carry

    lax.fori_loop(0, width // column, step, 0)


def whole_product(scalars, pieces, ws, contract, outs, n, name):
    width = ws[0].shape[2 if contract == 0 else 1]
    hidden = ws[0].shape[1 if contract == 0 else 2]
    rows = pieces[0].shape[1]
    return whole_call(
        functools.partial(whole_kernel, len(pieces), outs, hidden // n, contract),
        [jax.ShapeDtypeStruct((rows // outs, width), BF16)] * outs,
        [],
        2 * rows * width * hidden * len(ws),
        2 * (rows * width + hidden * width * len(ws)),
        name,
        scalars,
        *pieces,
        *ws,
    )


def sum_blocks(make, n):
    held = n // 2
    sent = make(held, held)
    addends = [swap(sent, "dp", 1), make(0, held)]
    mask = 2
    while mask < n:
        held //= 2
        leaving = sum(a[held:].astype(F32) for a in addends).astype(BF16)
        addends = [a[:held] for a in addends] + [swap(leaving, "dp", mask)]
        mask *= 2
    return sum(a[0].astype(F32) for a in addends)


def spread_blocks(mine, n):
    pieces = [mine[None]]
    mask = n // 2
    while mask:
        pieces.append(swap(pieces[0] if len(pieces) == 1 else jnp.concatenate(pieces, axis=0), "dp", mask))
        mask //= 2
    return pieces


def local_paired(tokens, expert_ids, gate_probs, w_gate, w_up, w_down, out_grad):
    experts, n = lax.axis_size("ep"), lax.axis_size("dp")
    chips = experts // 2
    group_len = expert_ids.shape[0]
    capacity = 3 * ((group_len * TOP + 2 * experts - 1) // (2 * experts))
    z = lax.axis_index("dp")
    scalars = jnp.stack([lax.axis_index("ep")] + [z ^ p for p in order(n)]).astype(jnp.int32)
    meta = jnp.concatenate([expert_ids.T.astype(F32), gate_probs.T], axis=0)
    meta_away = swap(meta, "ep", 1)

    def send_out(x, weighted):
        arrived = gather_rows(scalars, (meta, meta_away), (x, swap(x, "ep", 1)), chips, capacity, weighted)
        return [swap(part, "ep", 2 * k) if k else part for k, part in enumerate(arrived)]

    rows = send_out(tokens, False)
    grads = send_out(out_grad, True)

    sets = [tuple(k for k in ks if k < chips) for ks in ROW_SETS]
    sums = []
    for ks in sets:
        sums.append(
            sum_blocks(
                lambda first, count: part_blocks(
                    scalars, [rows[k] for k in ks], [w_gate, w_up], 0, first, count, n, "gate_up"
                ),
                n,
            )
        )
    hidden_pieces, back = [], []
    block = w_gate.shape[2] // n
    for ks, total in zip(sets, sums):
        gate, up = total[:, :block], total[:, block:]
        sigmoid = jax.nn.sigmoid(gate)
        hidden_pieces.append(spread_blocks((gate * sigmoid * up).astype(BF16), n))
    for ks, total in zip(sets, sums):
        gate, up = total[:, :block], total[:, block:]
        d_hidden = sum_blocks(
            lambda first, count: part_blocks(
                scalars, [grads[k] for k in ks], [w_down], 1, first, count, n, "d_hidden"
            ),
            n,
        )
        sigmoid = jax.nn.sigmoid(gate)
        d_gate = d_hidden * up * sigmoid * (1.0 + gate * (1.0 - sigmoid))
        d_up = d_hidden * (gate * sigmoid)
        back.append(jnp.concatenate([d_gate, d_up], axis=1).astype(BF16))

    def bring_back(ks, made):
        return {k: swap(m, "ep", 2 * k) if k else m for k, m in zip(ks, made)}

    out_back, in_back = {}, {}
    for ks, pieces in reversed(list(zip(sets, hidden_pieces))):
        made = whole_product(scalars, pieces, [w_down], 0, len(ks), n, "expert_out")
        out_back.update(bring_back(ks, made))
    for ks, mine in reversed(list(zip(sets, back))):
        made = whole_product(scalars, spread_blocks(mine, n), [w_gate, w_up], 1, len(ks), n, "input_out")
        in_back.update(bring_back(ks, made))

    def finish(returned, weighted):
        returned = [returned[k] for k in range(chips)]
        away = combine_rows(scalars, meta_away, returned, capacity, 1, weighted, BF16)
        came = swap(away, "ep", 1)
        own = combine_rows(scalars, meta, returned, capacity, 0, weighted, F32)
        return (own + came.astype(F32)).astype(BF16)

    return finish(out_back, True), finish(in_back, False)


def paired(experts, n, group_len, hidden):
    capacity = 3 * ((group_len * TOP + 2 * experts - 1) // (2 * experts))
    whole = experts & (experts - 1) == 0 and n & (n - 1) == 0 and min(experts, n) > 1
    return whole and experts <= 8 and hidden % (128 * n) == 0 and capacity % 16 == 0


def local(tokens, expert_ids, gate_probs, w_gate, w_up, w_down, out_grad):
    fits = paired(lax.axis_size("ep"), lax.axis_size("dp"), expert_ids.shape[0], w_gate.shape[2])
    step = local_paired if fits else local_any
    return step(tokens, expert_ids, gate_probs, w_gate, w_up, w_down, out_grad)


def solution(mesh):
    return jax.shard_map(
        local,
        mesh=mesh,
        in_specs=(
            P("ep", "dp"),
            P("ep", None),
            P("ep", None),
            P("ep", "dp", None),
            P("ep", "dp", None),
            P("ep", None, "dp"),
            P("ep", "dp"),
        ),
        out_specs=(P("ep", "dp"), P("ep", "dp")),
        check_vma=False,
    )
```
